32 devices in a mesh: ctx: 4 (over z), exp: 8 (over y, x, core).
Axes of the slice: x: 2, y: 2, z: 4, core: 2. Of those that a mesh axis runs over, the one named last changes fastest.
Arguments:
- out_grad: bfloat16 [4096, 2048], P(('ctx', 'exp')), may hold values from -6 to 6
- route_ids: int32 [4096, 4], P(('ctx', 'exp')), may hold values from 0 to 15, all different within a row; in each aligned block of 128 rows (0 to 127, 128 to 255, ...) at most 36 rows name the same one
- gate_probs: float32 [4096, 4], P(('ctx', 'exp')), may hold values from 0 to 1, as said below
- saved_hidden: bfloat16 [4, 8, 16, 36, 768], P('ctx', None, 'exp'), may hold values from -6 to 6
- down_weight: bfloat16 [16, 768, 2048], P('exp', None, 'ctx'), may hold values from -0.02734375 to 0.02734375
- router_weight: bfloat16 [2048, 16], replicated, may hold values from -1.5 to 1.5
- proj_weight: bfloat16 [4096, 2048], P('ctx'), may hold values from -0.125 to 0.125
Outputs:
- head_grads: bfloat16 [4, 1024, 4096], P(None, 'exp', 'ctx')
- router_grad: float32 [4096, 4], P(('ctx', 'exp'))
The draws below stay inside these ranges and needn't reach their ends.
Inputs may be any that keep to these rules, and one draw needn't show every extreme that they name: `route_ids`: each token names 4 different experts; among the tokens of one device no expert is named more than 36 times, and in some device some expert is named exactly 36 times. `gate_probs`: positive; a token's 4 gates sum to one.
All inputs are finite; a program needn't handle non-finite values.
Results may differ from the reference program's by a relative error of at most 0.009.
Values may be sent and summed in bfloat16 or wider, within the bound.
A program may use at most 64 MiB of HBM per device.

```python
import math
import jax
import jax.numpy as jnp
import numpy as np
from jax import lax

D = 2048
FF = 768
HEADS = 32
HEAD_DIM = 128
TOP_K = 4
TOK_DEV = 128
EXPERTS = 16
CAPACITY = 36
TOKENS = 4096
N_CTX = 4
N_EXP = 8


def draw_gate_probs(key, part):
    logits = jax.random.normal(key, (TOKENS, TOP_K), jnp.float32)
    return jax.nn.softmax(logits, axis=-1).astype(jnp.float32)


def levels(own_key, dims, split, least, top_value):
    gain, own = 1.0, jax.random.fold_in(own_key, 6)
    for dim, shards_of in split:
        steps = jnp.exp(jax.random.uniform(jax.random.fold_in(own, dim), (shards_of,), jnp.float32, least / len(split), top_value / len(split)))
        gain = gain * jnp.repeat(steps, dims[dim] // shards_of).reshape([-1 if axis == dim else 1 for axis in range(len(dims))])
    return gain


def deal_out(own_key, own, number, rows, amount, top, reach, skew):
    sequence = jax.random.permutation(own_key, amount)
    heavy_load, usual = portions_of(amount, rows * top, reach, skew, True), portions_of(amount, rows * top, reach, skew, False)
    places = jnp.arange(amount)

    def named(lengths, offset_by):
        used = int((lengths > 0).sum())
        fixed = max(1, used // 4)
        shifted = fixed + (places - fixed + offset_by * (used - fixed)) % max(1, amount - fixed)
        return jnp.zeros((amount,), jnp.int32).at[sequence[jnp.where(places < fixed, places, shifted)]].set(jnp.asarray(lengths, jnp.int32))

    lengths = jnp.where(number % 4 == 0, named(heavy_load, number // 4), named(usual, number - number // 4 - 1))
    mixed = jax.random.permutation(jax.random.fold_in(own, 3), amount)
    donor, taker = mixed[0:amount // 2 * 2:2], mixed[1:amount // 2 * 2:2]
    room = jnp.minimum(lengths[donor] - 1, reach - lengths[taker]) // 2
    room = jnp.where((donor == sequence[0]) | (taker == sequence[0]) | (lengths[taker] == 0), 0, jnp.maximum(room, 0))
    shifted = jax.random.randint(jax.random.fold_in(own, 4), (amount // 2,), 0, 1 << 20) % (room + 1)
    lengths = lengths.at[donor].add(-shifted).at[taker].add(shifted)
    items = jnp.searchsorted(jnp.cumsum(lengths), jnp.arange(rows * top), side="right").astype(jnp.int32)
    table = items.reshape(top, rows).T
    table = table[jax.random.permutation(jax.random.fold_in(own, 1), rows)]
    offset_by = jax.random.randint(jax.random.fold_in(own, 2), (rows, 1), 0, top)
    return jnp.take_along_axis(table, (jnp.arange(top)[None, :] + offset_by) % top, axis=1)


def portions_of(number_of, total, most, skew, full):
    portions = [(1 << 20) // math.isqrt(grade ** skew) + 1 for grade in range(1, number_of + 1)]
    largest = most if full else min(most, max(-(-total // number_of), total * portions[0] // sum(portions)))
    least = 1 if total - largest >= number_of - 1 else 0
    counts, rest = [largest] + [least] * (number_of - 1), total - largest - least * (number_of - 1)
    while rest > 0:
        movable = [i for i in range(1, number_of) if counts[i] < largest] or [i for i in range(1, number_of) if counts[i] < most]
        whole, remaining = sum([portions[i] for i in movable]), rest
        for i in movable:
            addition = min(most - counts[i], max(1, remaining * portions[i] // whole), rest)
            counts[i] = counts[i] + addition
            rest = rest - addition
    return np.array(counts)


def bell_draw(key, shape, scale, most, split=(), kind=jnp.bfloat16):
    level = levels(key, shape, split, -0.22, 0.18) if split else 1.0
    entries = jax.random.normal(key, shape, jnp.float32) * scale * level
    return jnp.minimum(jnp.maximum(entries, -most), most).astype(kind)


def setup_inputs(seed: int = 0) -> dict:
    splits = jax.random.split(jax.random.key(seed), 8)
    out_grad = bell_draw(splits[0], (TOKENS, D), 1.0, 6.0, ((0, 32),))
    route_ids_keys = jax.random.split(jax.random.fold_in(splits[1], 1), TOKENS // TOK_DEV)
    route_ids_turns = jax.random.permutation(jax.random.fold_in(splits[1], 3), TOKENS // TOK_DEV)
    route_ids = jax.vmap(lambda own, number: deal_out(jax.random.fold_in(splits[1], 2), own, number, TOK_DEV, EXPERTS, TOP_K, CAPACITY, 2))(route_ids_keys, route_ids_turns).reshape((TOKENS, TOP_K))
    gate_probs = draw_gate_probs(jax.random.fold_in(splits[7], 71), 0)
    saved_hidden = bell_draw(splits[3], (N_CTX, N_EXP, EXPERTS, CAPACITY, FF), 1.0, 6.0, ((0, 4), (2, 8)))
    down_weight = bell_draw(splits[4], (EXPERTS, FF, D), (FF * 64) ** -0.5, 0.02734375, ((0, 8), (2, 4)))
    router_weight = bell_draw(splits[5], (D, EXPERTS), EXPERTS ** -0.5, 1.5)
    proj_weight = bell_draw(splits[6], (HEADS * HEAD_DIM, D), D ** -0.5, 0.125, ((0, 4),))
    return {"out_grad": out_grad, "route_ids": route_ids, "gate_probs": gate_probs, "saved_hidden": saved_hidden, "down_weight": down_weight, "router_weight": router_weight, "proj_weight": proj_weight}


def reference(out_grad, route_ids, gate_probs, saved_hidden, down_weight, router_weight, proj_weight):
    device_count = N_CTX * N_EXP
    per_device = route_ids.reshape(device_count, TOK_DEV * TOP_K)
    expert_range = jnp.arange(EXPERTS, dtype=jnp.int32)
    onehot = (per_device[:, :, None] == expert_range[None, None, :]).astype(jnp.int32)
    earlier = jnp.cumsum(onehot, axis=1) - onehot
    slot_rank = jnp.sum(earlier * onehot, axis=2).astype(jnp.int32).reshape(N_CTX, N_EXP, TOK_DEV, TOP_K)
    ids_group = route_ids.reshape(N_CTX, N_EXP, TOK_DEV, TOP_K)
    grad_group = out_grad.reshape(N_CTX, N_EXP, TOK_DEV, D)
    weight_wide = down_weight.astype(jnp.float32)
    sources = jnp.arange(N_EXP, dtype=jnp.int32)[:, None, None]

    def one_group(items):
        hidden, group_ids, ranks, grads = items
        recomputed = jnp.einsum("secf,efd->secd", hidden.astype(jnp.float32), weight_wide).astype(jnp.bfloat16)
        picked = recomputed[sources, group_ids, ranks]
        return jnp.sum(grads.astype(jnp.float32)[:, :, None, :] * picked.astype(jnp.float32), axis=3)

    gate_grad = lax.map(one_group, (saved_hidden, ids_group, slot_rank, grad_group)).reshape(TOKENS, TOP_K)
    weighted = jnp.sum(gate_probs * gate_grad, axis=1, keepdims=True)
    router_grad = gate_probs * (gate_grad - weighted)
    matches = route_ids[:, :, None] == expert_range[None, None, :]
    dense_grad = jnp.sum(jnp.where(matches, router_grad[:, :, None], jnp.zeros_like(router_grad)[:, :, None]), axis=1)
    router_term = jnp.dot(dense_grad, router_weight.astype(jnp.float32).T, precision=lax.Precision.HIGHEST)
    combined = (out_grad.astype(jnp.float32) + router_term).astype(jnp.bfloat16)
    head_flat = jnp.dot(combined, proj_weight.T, preferred_element_type=jnp.float32).astype(jnp.bfloat16)
    head_grads = head_flat.reshape(N_CTX, TOK_DEV * N_EXP, HEADS * HEAD_DIM)
    return head_grads, router_grad
```

```python
import jax
import jax.numpy as jnp
from jax import lax
from jax.sharding import PartitionSpec as P


def route_ranks(route_ids, experts):
    flat_ids = route_ids.reshape(-1)
    onehot = (flat_ids[:, None] == jnp.arange(experts, dtype=jnp.int32)[None, :]).astype(jnp.int32)
    earlier = jnp.cumsum(onehot, axis=0) - onehot
    slot_rank = jnp.sum(earlier * onehot, axis=1)
    return (flat_ids, slot_rank)


def shards(out_grad, route_ids, gate_probs, saved_hidden, down_weight, router_weight, proj_weight):
    tok_rows, top_count = route_ids.shape
    experts = router_weight.shape[1]
    groups = lax.axis_size("exp")
    n_ctx = lax.axis_size("ctx")
    local_experts = down_weight.shape[0]
    capacity = saved_hidden.shape[3]
    dslice = down_weight.shape[2]
    me_ctx = lax.axis_index("ctx")
    rows_all = lax.all_gather(out_grad, "ctx", axis=0, tiled=False)
    ids_all = lax.all_gather(route_ids, "ctx", axis=0, tiled=False)
    probs_all = lax.all_gather(gate_probs, "ctx", axis=0, tiled=False)
    hidden_all = lax.all_gather(saved_hidden[0], "ctx", axis=0, tiled=False)
    flat_ids, slot_rank = jax.vmap(lambda r: route_ranks(r, experts))(ids_all)
    positions = flat_ids * capacity + slot_rank
    cols = lax.dynamic_slice_in_dim(rows_all, me_ctx * dslice, dslice, axis=2)
    spread = jnp.repeat(cols, top_count, axis=1)
    blk = jnp.broadcast_to(jnp.arange(n_ctx, dtype=jnp.int32)[:, None], flat_ids.shape)
    send_rows = jnp.zeros(
        (groups, n_ctx, local_experts, capacity, dslice), out_grad.dtype
    ).at[flat_ids // local_experts, blk, flat_ids % local_experts, slot_rank].set(spread)
    arrived = lax.all_to_all(send_rows, "exp", split_axis=0, concat_axis=0, tiled=True)
    outputs = jnp.einsum(
        "csekf,efn->scekn", hidden_all, down_weight, preferred_element_type=jnp.float32
    ).astype(jnp.bfloat16)
    partial_grad = jnp.sum(arrived.astype(jnp.float32) * outputs.astype(jnp.float32), axis=4)
    returned = lax.all_to_all(partial_grad, "exp", split_axis=0, concat_axis=0, tiled=True)
    returned = lax.psum(returned, "ctx")
    returned = jnp.transpose(returned, (1, 0, 2, 3)).reshape(n_ctx, experts * capacity)
    gate_grad = jnp.take_along_axis(returned, positions, axis=1).reshape(n_ctx, tok_rows, top_count)
    weighted = jnp.sum(probs_all * gate_grad, axis=2, keepdims=True)
    router_all = probs_all * (gate_grad - weighted)
    matches = ids_all[:, :, :, None] == jnp.arange(experts, dtype=jnp.int32)[None, None, None, :]
    dense_all = jnp.sum(jnp.where(matches, router_all[:, :, :, None], 0.0), axis=2)
    router_wide = router_weight.astype(jnp.float32)
    combined = (
        rows_all.astype(jnp.float32)
        + lax.dot_general(
            dense_all, router_wide, (((2,), (1,)), ((), ())), precision=lax.Precision.HIGHEST
        )
    ).astype(jnp.bfloat16)
    head_flat = lax.dot_general(
        combined.reshape(n_ctx * tok_rows, -1),
        proj_weight,
        (((1,), (1,)), ((), ())),
        preferred_element_type=jnp.float32,
    ).astype(jnp.bfloat16)
    head_grads = head_flat.reshape(n_ctx, tok_rows, proj_weight.shape[0])
    router_grad = lax.dynamic_index_in_dim(router_all, me_ctx, axis=0, keepdims=False)
    return (head_grads, router_grad)


def solution(mesh):
    return jax.shard_map(
        shards,
        mesh=mesh,
        in_specs=(
            P(("ctx", "exp"), None),
            P(("ctx", "exp"), None),
            P(("ctx", "exp"), None),
            P("ctx", None, "exp", None, None),
            P("exp", None, "ctx"),
            P(),
            P("ctx", None),
        ),
        out_specs=(P(None, "exp", "ctx"), P(("ctx", "exp"), None)),
        check_vma=False,
    )
```

```python
import jax
import jax.numpy as jnp
from jax import lax
from jax.sharding import PartitionSpec as P


def route_ranks(route_ids, experts):
    flat_ids = route_ids.reshape(-1)
    onehot = (flat_ids[:, None] == jnp.arange(experts, dtype=jnp.int32)[None, :]).astype(jnp.int32)
    earlier = jnp.cumsum(onehot, axis=0) - onehot
    slot_rank = jnp.sum(earlier * onehot, axis=1)
    return (flat_ids, slot_rank)


def shards(out_grad, route_ids, gate_probs, saved_hidden, down_weight, router_weight, proj_weight):
    tok_rows, top_count = route_ids.shape
    experts = router_weight.shape[1]
    groups = lax.axis_size("exp")
    n_ctx = lax.axis_size("ctx")
    local_experts = down_weight.shape[0]
    capacity = saved_hidden.shape[3]
    dslice = down_weight.shape[2]
    me_ctx = lax.axis_index("ctx")
    rows_all = lax.all_gather(out_grad, "ctx", axis=0, tiled=False)
    packed = jnp.concatenate([route_ids.astype(jnp.float32), gate_probs], axis=1)
    packed_all = lax.all_gather(packed, "ctx", axis=0, tiled=False)
    ids_all = packed_all[:, :, :top_count].astype(jnp.int32)
    probs_all = packed_all[:, :, top_count:]
    hidden_all = lax.all_gather(saved_hidden[0], "ctx", axis=0, tiled=False)
    flat_ids, slot_rank = jax.vmap(lambda r: route_ranks(r, experts))(ids_all)
    positions = flat_ids * capacity + slot_rank
    cols = lax.dynamic_slice_in_dim(rows_all, me_ctx * dslice, dslice, axis=2)
    spread = jnp.repeat(cols, top_count, axis=1)
    blk = jnp.broadcast_to(jnp.arange(n_ctx, dtype=jnp.int32)[:, None], flat_ids.shape)
    send_rows = jnp.zeros(
        (groups, n_ctx, local_experts, capacity, dslice), out_grad.dtype
    ).at[flat_ids // local_experts, blk, flat_ids % local_experts, slot_rank].set(spread)
    arrived = lax.all_to_all(send_rows, "exp", split_axis=0, concat_axis=0, tiled=True)
    outputs = jnp.einsum(
        "csekf,efn->scekn", hidden_all, down_weight, preferred_element_type=jnp.float32
    ).astype(jnp.bfloat16)
    partial_grad = jnp.sum(arrived.astype(jnp.float32) * outputs.astype(jnp.float32), axis=4)
    returned = lax.all_to_all(partial_grad, "exp", split_axis=0, concat_axis=0, tiled=True)
    returned = lax.psum(returned, "ctx")
    returned = jnp.transpose(returned, (1, 0, 2, 3)).reshape(n_ctx, experts * capacity)
    picks = positions[:, :, None] == jnp.arange(experts * capacity, dtype=jnp.int32)[None, None, :]
    gate_grad = jnp.sum(jnp.where(picks, returned[:, None, :], 0.0), axis=2)
    gate_grad = gate_grad.reshape(n_ctx, tok_rows, top_count)
    weighted = jnp.sum(probs_all * gate_grad, axis=2, keepdims=True)
    router_all = probs_all * (gate_grad - weighted)
    matches = ids_all[:, :, :, None] == jnp.arange(experts, dtype=jnp.int32)[None, None, None, :]
    dense_all = jnp.sum(jnp.where(matches, router_all[:, :, :, None], 0.0), axis=2)
    router_wide = router_weight.astype(jnp.float32)
    combined = (
        rows_all.astype(jnp.float32)
        + lax.dot_general(
            dense_all, router_wide, (((2,), (1,)), ((), ())), precision=lax.Precision.HIGHEST
        )
    ).astype(jnp.bfloat16)
    head_flat = lax.dot_general(
        combined.reshape(n_ctx * tok_rows, -1),
        proj_weight,
        (((1,), (1,)), ((), ())),
        preferred_element_type=jnp.float32,
    ).astype(jnp.bfloat16)
    head_grads = head_flat.reshape(n_ctx, tok_rows, proj_weight.shape[0])
    router_grad = lax.dynamic_index_in_dim(router_all, me_ctx, axis=0, keepdims=False)
    return (head_grads, router_grad)


def solution(mesh):
    return jax.shard_map(
        shards,
        mesh=mesh,
        in_specs=(
            P(("ctx", "exp"), None),
            P(("ctx", "exp"), None),
            P(("ctx", "exp"), None),
            P("ctx", None, "exp", None, None),
            P("exp", None, "ctx"),
            P(),
            P("ctx", None),
        ),
        out_specs=(P(None, "exp", "ctx"), P(("ctx", "exp"), None)),
        check_vma=False,
    )
```

```python
import jax
import jax.numpy as jnp
from jax import lax
from jax.sharding import PartitionSpec as P


def route_ranks(route_ids, experts):
    flat_ids = route_ids.reshape(-1)
    onehot = (flat_ids[:, None] == jnp.arange(experts, dtype=jnp.int32)[None, :]).astype(jnp.int32)
    earlier = jnp.cumsum(onehot, axis=0) - onehot
    slot_rank = jnp.sum(earlier * onehot, axis=1)
    return (flat_ids, slot_rank)


def shards(out_grad, route_ids, gate_probs, saved_hidden, down_weight, router_weight, proj_weight):
    tok_rows, top_count = route_ids.shape
    experts = router_weight.shape[1]
    groups = lax.axis_size("exp")
    n_ctx = lax.axis_size("ctx")
    local_experts = down_weight.shape[0]
    capacity = saved_hidden.shape[3]
    dslice = down_weight.shape[2]
    me_ctx = lax.axis_index("ctx")
    rows_all = lax.all_gather(out_grad, "ctx", axis=0, tiled=False)
    packed = jnp.concatenate([route_ids.astype(jnp.float32), gate_probs], axis=1)
    packed_all = lax.all_gather(packed, "ctx", axis=0, tiled=False)
    ids_all = packed_all[:, :, :top_count].astype(jnp.int32)
    probs_all = packed_all[:, :, top_count:]
    own = saved_hidden[0]
    right, left, from_left, from_right = own, own, [], []
    for _ in range(n_ctx - 1):
        right = lax.ppermute(right, "ctx", [(i, i + 1) for i in range(n_ctx - 1)])
        left = lax.ppermute(left, "ctx", [(i + 1, i) for i in range(n_ctx - 1)])
        from_left.append(right)
        from_right.append(left)
    hidden_all = jnp.zeros((n_ctx,) + own.shape, own.dtype)
    for k in range(n_ctx - 1, 0, -1):
        hidden_all = lax.dynamic_update_index_in_dim(hidden_all, from_left[k - 1], jnp.maximum(me_ctx - k, 0), 0)
    for k in range(n_ctx - 1, 0, -1):
        hidden_all = lax.dynamic_update_index_in_dim(hidden_all, from_right[k - 1], jnp.minimum(me_ctx + k, n_ctx - 1), 0)
    hidden_all = lax.dynamic_update_index_in_dim(hidden_all, own, me_ctx, 0)
    flat_ids, slot_rank = jax.vmap(lambda r: route_ranks(r, experts))(ids_all)
    positions = flat_ids * capacity + slot_rank
    cols = lax.dynamic_slice_in_dim(rows_all, me_ctx * dslice, dslice, axis=2)
    spread = jnp.repeat(cols, top_count, axis=1)
    blk = jnp.broadcast_to(jnp.arange(n_ctx, dtype=jnp.int32)[:, None], flat_ids.shape)
    send_rows = jnp.zeros(
        (groups, n_ctx, local_experts, capacity, dslice), out_grad.dtype
    ).at[flat_ids // local_experts, blk, flat_ids % local_experts, slot_rank].set(spread)
    arrived = lax.all_to_all(send_rows, "exp", split_axis=0, concat_axis=0, tiled=True)
    outputs = jnp.einsum(
        "csekf,efn->scekn", hidden_all, down_weight, preferred_element_type=jnp.float32
    ).astype(jnp.bfloat16)
    partial_grad = jnp.sum(arrived.astype(jnp.float32) * outputs.astype(jnp.float32), axis=4)
    returned = lax.all_to_all(partial_grad, "exp", split_axis=0, concat_axis=0, tiled=True)
    returned = lax.psum(returned, "ctx")
    returned = jnp.transpose(returned, (1, 0, 2, 3)).reshape(n_ctx, experts * capacity)
    picks = positions[:, :, None] == jnp.arange(experts * capacity, dtype=jnp.int32)[None, None, :]
    gate_grad = jnp.sum(jnp.where(picks, returned[:, None, :], 0.0), axis=2)
    gate_grad = gate_grad.reshape(n_ctx, tok_rows, top_count)
    weighted = jnp.sum(probs_all * gate_grad, axis=2, keepdims=True)
    router_all = probs_all * (gate_grad - weighted)
    matches = ids_all[:, :, :, None] == jnp.arange(experts, dtype=jnp.int32)[None, None, None, :]
    dense_all = jnp.sum(jnp.where(matches, router_all[:, :, :, None], 0.0), axis=2)
    router_wide = router_weight.astype(jnp.float32)
    combined = (
        rows_all.astype(jnp.float32)
        + lax.dot_general(
            dense_all, router_wide, (((2,), (1,)), ((), ())), precision=lax.Precision.HIGHEST
        )
    ).astype(jnp.bfloat16)
    head_flat = lax.dot_general(
        combined.reshape(n_ctx * tok_rows, -1),
        proj_weight,
        (((1,), (1,)), ((), ())),
        preferred_element_type=jnp.float32,
    ).astype(jnp.bfloat16)
    head_grads = head_flat.reshape(n_ctx, tok_rows, proj_weight.shape[0])
    router_grad = lax.dynamic_index_in_dim(router_all, me_ctx, axis=0, keepdims=False)
    return (head_grads, router_grad)


def solution(mesh):
    return jax.shard_map(
        shards,
        mesh=mesh,
        in_specs=(
            P(("ctx", "exp"), None),
            P(("ctx", "exp"), None),
            P(("ctx", "exp"), None),
            P("ctx", None, "exp", None, None),
            P("exp", None, "ctx"),
            P(),
            P("ctx", None),
        ),
        out_specs=(P(None, "exp", "ctx"), P(("ctx", "exp"), None)),
        check_vma=False,
    )
```

```python
import jax
import jax.numpy as jnp
from jax import lax
from jax.sharding import PartitionSpec as P


def route_ranks(route_ids, experts):
    flat_ids = route_ids.reshape(-1)
    onehot = (flat_ids[:, None] == jnp.arange(experts, dtype=jnp.int32)[None, :]).astype(jnp.int32)
    earlier = jnp.cumsum(onehot, axis=0) - onehot
    slot_rank = jnp.sum(earlier * onehot, axis=1)
    return (flat_ids, slot_rank)


def shards(out_grad, route_ids, gate_probs, saved_hidden, down_weight, router_weight, proj_weight):
    tok_rows, top_count = route_ids.shape
    experts = router_weight.shape[1]
    groups = lax.axis_size("exp")
    n_ctx = lax.axis_size("ctx")
    local_experts = down_weight.shape[0]
    capacity = saved_hidden.shape[3]
    dslice = down_weight.shape[2]
    me_ctx = lax.axis_index("ctx")
    rows_all = lax.all_gather(out_grad, "ctx", axis=0, tiled=False)
    packed = jnp.concatenate([route_ids.astype(jnp.float32), gate_probs], axis=1)
    packed_all = lax.all_gather(packed, "ctx", axis=0, tiled=False)
    ids_all = packed_all[:, :, :top_count].astype(jnp.int32)
    probs_all = packed_all[:, :, top_count:]
    hidden_all = lax.all_gather(saved_hidden[0], "ctx", axis=0, tiled=False)
    flat_ids, slot_rank = jax.vmap(lambda r: route_ranks(r, experts))(ids_all)
    positions = flat_ids * capacity + slot_rank
    cols = lax.dynamic_slice_in_dim(rows_all, me_ctx * dslice, dslice, axis=2)
    spread = jnp.repeat(cols, top_count, axis=1)
    blk = jnp.broadcast_to(jnp.arange(n_ctx, dtype=jnp.int32)[:, None], flat_ids.shape)
    send_rows = jnp.zeros(
        (groups, n_ctx, local_experts, capacity, dslice), out_grad.dtype
    ).at[flat_ids // local_experts, blk, flat_ids % local_experts, slot_rank].set(spread)
    arrived = lax.all_to_all(send_rows, "exp", split_axis=0, concat_axis=0, tiled=True)
    outputs = jnp.einsum(
        "csekf,efn->scekn", hidden_all, down_weight, preferred_element_type=jnp.float32
    ).astype(jnp.bfloat16)
    partial_grad = jnp.sum(arrived.astype(jnp.float32) * outputs.astype(jnp.float32), axis=4)
    returned = lax.all_to_all(partial_grad, "exp", split_axis=0, concat_axis=0, tiled=True)
    returned = jnp.sum(lax.all_gather(returned, "ctx", axis=0, tiled=False), axis=0)
    returned = jnp.transpose(returned, (1, 0, 2, 3)).reshape(n_ctx, experts * capacity)
    picks = positions[:, :, None] == jnp.arange(experts * capacity, dtype=jnp.int32)[None, None, :]
    gate_grad = jnp.sum(jnp.where(picks, returned[:, None, :], 0.0), axis=2)
    gate_grad = gate_grad.reshape(n_ctx, tok_rows, top_count)
    weighted = jnp.sum(probs_all * gate_grad, axis=2, keepdims=True)
    router_all = probs_all * (gate_grad - weighted)
    matches = ids_all[:, :, :, None] == jnp.arange(experts, dtype=jnp.int32)[None, None, None, :]
    dense_all = jnp.sum(jnp.where(matches, router_all[:, :, :, None], 0.0), axis=2)
    router_wide = router_weight.astype(jnp.float32)
    combined = (
        rows_all.astype(jnp.float32)
        + lax.dot_general(
            dense_all, router_wide, (((2,), (1,)), ((), ())), precision=lax.Precision.HIGHEST
        )
    ).astype(jnp.bfloat16)
    head_flat = lax.dot_general(
        combined.reshape(n_ctx * tok_rows, -1),
        proj_weight,
        (((1,), (1,)), ((), ())),
        preferred_element_type=jnp.float32,
    ).astype(jnp.bfloat16)
    head_grads = head_flat.reshape(n_ctx, tok_rows, proj_weight.shape[0])
    router_grad = lax.dynamic_index_in_dim(router_all, me_ctx, axis=0, keepdims=False)
    return (head_grads, router_grad)


def solution(mesh):
    return jax.shard_map(
        shards,
        mesh=mesh,
        in_specs=(
            P(("ctx", "exp"), None),
            P(("ctx", "exp"), None),
            P(("ctx", "exp"), None),
            P("ctx", None, "exp", None, None),
            P("exp", None, "ctx"),
            P(),
            P("ctx", None),
        ),
        out_specs=(P(None, "exp", "ctx"), P(("ctx", "exp"), None)),
        check_vma=False,
    )
```
